256 devices in a mesh: dp: 8 (over z), seq: 32 (over x, y, core).
Axes of the slice: x: 4, y: 4, z: 8, core: 2. Of those that a mesh axis runs over, the one named last changes fastest.
Arguments:
- tokens: bfloat16 [8, 12288, 4096], P('dp', 'seq'), may hold values from -16 to 16
- qkv_weight: bfloat16 [4096, 3072], P(('dp', 'seq')), may hold values from -1 to 1
- segments: int32 [8, 12288], P('dp', 'seq'), may hold values from 0 to 12287, as said below
- destination: int32 [8, 12288], P('dp', 'seq'), may hold values from 0 to 12287, as said below
- doc_prefix: int32 [8, 32], P('dp', 'seq'), may hold values from 0 to 768, as said below
Outputs:
- attended: bfloat16 [8, 12288, 2048], P('dp', 'seq')
The draws below stay inside these ranges and needn't reach their ends.
Inputs may be any that keep to these rules, and one draw needn't show every extreme that they name: `segments`: A token's id is the position in its sequence of its document's first token, so ids never fall and start at 0; the last token of every sequence is a document of its own. doc_prefix[b, d] is the number of tokens before row d * 384 of sequence b with that row's segment id; the most is reached in every draw. `destination`: each row is a permutation; the tokens of one device go to exactly 16 devices of the sequence, exactly 24 to each, and every device receives tokens from exactly 16 devices.
All inputs are finite; a program needn't handle non-finite values.
Results may differ from the reference program's by a relative error of at most 0.012.
The reference program's roundings to bfloat16 on the way (of `probs` and `heads_out`) count: a program that leaves them out, or rounds other values in their place, can miss the bound.
Values may be sent and summed in bfloat16 or wider, within the bound.
No kernel may reach another device: no remote copies, remote signals or barrier semaphores. Data moves between devices by JAX's collectives and lax.ppermute only.
A program may use at most 128 MiB of HBM per device.

```python
import jax
import jax.numpy as jnp
from jax import lax

D = 4096
HEADS = 16
KV_HEADS = 4
HEAD_DIM = 128
TOK_DEV = 384
REACH = 2
GROUPS = 16
CAP = 24
SEQ_LEN = 12288
BATCH = 8
QKV = 3072
N_SEQ = 32


def document_flags(key):

    def draw_row(row_key):
        subkeys = jax.random.split(row_key, 3)
        index_list = jnp.arange(SEQ_LEN, dtype=jnp.int32)
        doc_flags = jax.random.randint(subkeys[0], (SEQ_LEN,), 0, 48) == 0
        anchor = jax.random.randint(subkeys[1], (), 0, N_SEQ - REACH)
        tail_len = jax.random.randint(subkeys[2], (), 1, TOK_DEV)
        device = index_list // TOK_DEV
        at_start = index_list % TOK_DEV == 0
        forced = at_start & ((device - anchor) % REACH == 0)
        doc_flags = doc_flags | forced | (index_list == 0)
        lower = anchor * TOK_DEV
        upper = (anchor + REACH) * TOK_DEV + tail_len
        doc_flags = jnp.where((index_list > lower) & (index_list < upper), False, doc_flags)
        return doc_flags | (index_list == lower) | (index_list == upper) | (index_list == SEQ_LEN - 1)
    return jax.vmap(draw_row)(jax.random.split(key, BATCH))


def document_starts(doc_flags):
    index_list = jnp.arange(SEQ_LEN, dtype=jnp.int32)
    return lax.cummax(jnp.where(doc_flags, index_list[None, :], 0), axis=1).astype(jnp.int32)


def draw_segments(key, part):
    doc_flags = document_flags(jax.random.fold_in(key, 11))
    return document_starts(doc_flags)


def draw_doc_prefix(key, part):
    doc_flags = document_flags(jax.random.fold_in(key, 11))
    doc_start = document_starts(doc_flags)
    starts = doc_start[:, ::TOK_DEV]
    return (jnp.arange(N_SEQ, dtype=jnp.int32)[None, :] * TOK_DEV - starts).astype(jnp.int32)


def draw_destination(key, part):

    def draw_row(row_key):
        subkeys = jax.random.split(row_key, 4)
        relabel = jax.random.permutation(subkeys[0], N_SEQ)
        inverse = jnp.argsort(relabel)
        shifts = jax.random.permutation(subkeys[1], N_SEQ)[:GROUPS]
        source_perm = jax.vmap(lambda inner: jax.random.permutation(inner, TOK_DEV))(jax.random.split(subkeys[2], N_SEQ))
        target_perm = jax.vmap(lambda inner: jax.random.permutation(inner, TOK_DEV))(jax.random.split(subkeys[3], N_SEQ))
        device = jnp.arange(N_SEQ, dtype=jnp.int32)[:, None]
        block_index = source_perm // CAP
        offset = source_perm % CAP
        target = inverse[(relabel[device] + shifts[block_index]) % N_SEQ]
        target_row = target_perm[target, block_index * CAP + offset]
        return (target * TOK_DEV + target_row).reshape(SEQ_LEN).astype(jnp.int32)
    return jax.vmap(draw_row)(jax.random.split(jax.random.fold_in(key, 41), BATCH))


def draw_tokens(key, part):
    subkeys = jax.random.split(jax.random.fold_in(key, 21), 1)
    values = jax.random.normal(subkeys[0], (BATCH, SEQ_LEN, D))
    return jnp.clip(values, -16.0, 16.0).astype(jnp.bfloat16)


def draw_qkv_weight(key, part):
    subkeys = jax.random.split(jax.random.fold_in(key, 31), 1)
    values = jax.random.normal(subkeys[0], (D, QKV)) * D ** (-0.5)
    return jnp.clip(values, -1.0, 1.0).astype(jnp.bfloat16)


def setup_inputs(seed: int = 0) -> dict:
    keys = jax.random.split(jax.random.key(seed), 6)
    tokens = draw_tokens(jax.random.fold_in(keys[5], 71), 0)
    qkv_weight = draw_qkv_weight(jax.random.fold_in(keys[5], 71), 0)
    segments = draw_segments(jax.random.fold_in(keys[5], 71), 0)
    destination = draw_destination(jax.random.fold_in(keys[5], 71), 0)
    doc_prefix = draw_doc_prefix(jax.random.fold_in(keys[5], 71), 0)
    return dict(tokens=tokens, qkv_weight=qkv_weight, segments=segments, destination=destination, doc_prefix=doc_prefix)


ROPE_BASE = 500000.0
MASKED = -1.0e30


def positions(segment_ids, prefix_len):
    index_list = jnp.arange(segment_ids.shape[0], dtype=jnp.int32)
    fresh_doc = jnp.concatenate([jnp.ones((1,), jnp.bool_), segment_ids[1:] != segment_ids[:-1]])
    first_row = lax.cummax(jnp.where(fresh_doc, index_list, 0), axis=0)
    leading = segment_ids == segment_ids[0]
    position = index_list - first_row + jnp.where(leading, prefix_len, 0)
    return position, leading


def rotate(heads, position):
    half_dim = heads.shape[-1] // 2
    frequency = ROPE_BASE ** (-2.0 * jnp.arange(half_dim, dtype=jnp.float32) / heads.shape[-1])
    angles = position.astype(jnp.float32)[:, None] * frequency[None, :]
    cosine = jnp.cos(angles)[:, None, :]
    sine = jnp.sin(angles)[:, None, :]
    first_half = heads[..., :half_dim]
    second_half = heads[..., half_dim:]
    return jnp.concatenate([first_half * cosine - second_half * sine, second_half * cosine + first_half * sine], axis=-1)


def visible_keys(segment_ids, leading, prefix_len, reach):
    count = segment_ids.shape[0]
    query_rows = jnp.arange(count, dtype=jnp.int32)
    columns = jnp.arange((reach + 1) * count, dtype=jnp.int32) - reach * count
    key_segments = jnp.concatenate([jnp.full((reach * count,), -1, jnp.int32), segment_ids])
    local_part = (columns[None, :] >= 0) & (columns[None, :] <= query_rows[:, None]) & (key_segments[None, :] == segment_ids[:, None])
    remote_part = (columns[None, :] < 0) & (columns[None, :] >= -prefix_len) & leading[:, None]
    return local_part | remote_part


def attend(queries, keys_rot, values, key_mask):
    query_f = queries.astype(jnp.float32)
    key_f = keys_rot.astype(jnp.float32)
    value_f = values.astype(jnp.float32)
    scores = jnp.einsum("tkgd,lkd->kgtl", query_f, key_f) * (HEAD_DIM ** -0.5)
    scores = jnp.where(key_mask[None, None], scores, MASKED)
    top_score = jnp.max(scores, axis=-1, keepdims=True)
    expo = jnp.exp(scores - top_score)
    row_total = jnp.sum(expo, axis=-1, keepdims=True)
    probs = (expo / row_total).astype(jnp.bfloat16)
    heads_out = jnp.einsum("kgtl,lkd->tkgd", probs.astype(jnp.float32), value_f)
    return heads_out.reshape(queries.shape[0], HEADS * HEAD_DIM).astype(jnp.bfloat16)


def one_sequence(weight, packed):
    token_rows, segment_row, target_row, prefix_row = packed
    query_width = HEADS * HEAD_DIM
    kv_width = KV_HEADS * HEAD_DIM
    group_size = HEADS // KV_HEADS
    projected = jnp.dot(token_rows, weight, preferred_element_type=jnp.float32)
    position, leading = jax.vmap(positions)(segment_row.reshape(N_SEQ, TOK_DEV), prefix_row)
    position = position.reshape(SEQ_LEN)
    leading = leading.reshape(SEQ_LEN)
    queries = rotate(projected[:, :query_width].reshape(SEQ_LEN, HEADS, HEAD_DIM), position).astype(jnp.bfloat16)
    keys_rot = rotate(projected[:, query_width:query_width + kv_width].reshape(SEQ_LEN, KV_HEADS, HEAD_DIM), position).astype(jnp.bfloat16)
    values = projected[:, query_width + kv_width:].reshape(SEQ_LEN, KV_HEADS, HEAD_DIM).astype(jnp.bfloat16)
    front_pad = REACH * TOK_DEV
    keys_pad = jnp.concatenate([jnp.zeros((front_pad, KV_HEADS, HEAD_DIM), jnp.bfloat16), keys_rot], axis=0)
    values_pad = jnp.concatenate([jnp.zeros((front_pad, KV_HEADS, HEAD_DIM), jnp.bfloat16), values], axis=0)

    def per_device(device):
        row_start = (device * TOK_DEV).astype(jnp.int32)
        query_block = lax.dynamic_slice_in_dim(queries, row_start, TOK_DEV, 0).reshape(TOK_DEV, KV_HEADS, group_size, HEAD_DIM)
        key_block = lax.dynamic_slice_in_dim(keys_pad, row_start, front_pad + TOK_DEV, 0)
        value_block = lax.dynamic_slice_in_dim(values_pad, row_start, front_pad + TOK_DEV, 0)
        segment_block = lax.dynamic_slice_in_dim(segment_row, row_start, TOK_DEV, 0)
        leading_block = lax.dynamic_slice_in_dim(leading, row_start, TOK_DEV, 0)
        key_mask = visible_keys(segment_block, leading_block, prefix_row[device], REACH)
        return attend(query_block, key_block, value_block, key_mask)

    heads_out = lax.map(per_device, jnp.arange(N_SEQ, dtype=jnp.int32)).reshape(SEQ_LEN, query_width)
    return jnp.zeros_like(heads_out).at[target_row].set(heads_out)


def reference(tokens, qkv_weight, segments, destination, doc_prefix):
    def run_one(packed):
        return one_sequence(qkv_weight, packed)

    return lax.map(run_one, (tokens, segments, destination, doc_prefix))
```

```python
import functools

import jax
import jax.numpy as jnp
from jax import lax
from jax.experimental import pallas as pl
from jax.experimental.pallas import tpu as pltpu
from jax.sharding import Mesh, PartitionSpec as P

HEADS = 16
KV_HEADS = 4
HEAD_DIM = 128
REACH = 2
ROPE_BASE = 500000.0
MASKED = -1e30
LOG2E = 1.4426950408889634

NZ, NX, NY, NC = 8, 4, 4, 2
NCHIP = NX * NY
TOK = 384
CAP = 24
D = 4096
DEV = NCHIP * NC
PART = 512


bf16 = jnp.bfloat16
f32 = jnp.float32


def shift(x, axis, n, d):
    return lax.ppermute(x, axis, [(i, (i + d) % n) for i in range(n)])


def positions(segment_ids, prefix_len):
    index_list = jnp.arange(segment_ids.shape[0], dtype=jnp.int32)
    fresh_doc = jnp.concatenate([jnp.ones((1,), jnp.bool_), segment_ids[1:] != segment_ids[:-1]])
    first_row = lax.cummax(jnp.where(fresh_doc, index_list, 0), axis=0)
    leading = segment_ids == segment_ids[0]
    return index_list - first_row + jnp.where(leading, prefix_len, 0)


def project_kernel(rotary, zs_ref, own_ref, other_ref, w_ref, cos_ref, sin_ref, out_ref, acc_ref):
    step = pl.program_id(0)
    depth = own_ref.shape[1]
    w = w_ref[...].reshape(depth, PART)

    @pl.when(step == 0)
    def _():
        acc_ref[0] = jnp.dot(own_ref[...], w, preferred_element_type=f32)
        acc_ref[1] = jnp.dot(other_ref[...], w, preferred_element_type=f32)

    @pl.when(step > 0)
    def _():
        acc_ref[0] += jnp.dot(own_ref[...], w, preferred_element_type=f32)
        acc_ref[1] += jnp.dot(other_ref[...], w, preferred_element_type=f32)

    @pl.when(step == pl.num_programs(0) - 1)
    def _():
        for b in range(2):
            for h in range(PART // HEAD_DIM):
                cols = slice(h * HEAD_DIM, (h + 1) * HEAD_DIM)
                x = acc_ref[b, :, cols]
                if h < rotary:
                    x = x * cos_ref[b] + pltpu.roll(x, HEAD_DIM // 2, 1) * sin_ref[b]
                out_ref[b, :, cols] = x.astype(bf16)


def project(own, other, w, zs, cosine, sine, rotary):
    depth = D // NZ
    if w.ndim == 4:
        w_spec = pl.BlockSpec((NCHIP, 1, depth // NCHIP, PART), lambda s, zs: (0, s, 0, 0))
    else:
        w_spec = pl.BlockSpec((1, depth, PART), lambda s, zs: (s, 0, 0))
    tok_spec = pl.BlockSpec((TOK, depth), lambda s, zs: (0, zs[s]))
    whole = pl.BlockSpec((2, TOK, HEAD_DIM), lambda s, zs: (0, 0, 0))
    return pl.pallas_call(
        functools.partial(project_kernel, rotary),
        out_shape=jax.ShapeDtypeStruct((2, TOK, PART), bf16),
        grid_spec=pltpu.PrefetchScalarGridSpec(
            num_scalar_prefetch=1,
            grid=(NZ,),
            in_specs=[tok_spec, tok_spec, w_spec, whole, whole],
            out_specs=pl.BlockSpec((2, TOK, PART), lambda s, zs: (0, 0, 0)),
            scratch_shapes=[pltpu.VMEM((2, TOK, PART), f32)],
        ),
        compiler_params=pltpu.CompilerParams(dimension_semantics=("arbitrary",)),
        cost_estimate=pl.CostEstimate(
            flops=2 * 2 * TOK * D * PART, bytes_accessed=2 * (2 * TOK + PART) * D, transcendentals=0
        ),
        name="project",
    )(zs, own, other, w, cosine, sine)


def attend_kernel(
    head, info_ref, q_ref, cur_ref, prev_ref, segc_ref, segr_ref, slot_ref, out_ref, kv_ref, bias_ref, rows_ref
):
    core = info_ref[0]
    group = HEADS // KV_HEADS
    kc = slice(head * HEAD_DIM, (head + 1) * HEAD_DIM)
    vc = slice((2 + head) * HEAD_DIM, (3 + head) * HEAD_DIM)
    for n in range(2):
        i = jnp.bitwise_xor(core, n)
        kv_ref[n, :, :HEAD_DIM] = prev_ref[i, :, kc]
        kv_ref[n, :, HEAD_DIM:] = prev_ref[i, :, vc]
        kv_ref[2 + n, :, :HEAD_DIM] = cur_ref[i, :, kc]
        kv_ref[2 + n, :, HEAD_DIM:] = cur_ref[i, :, vc]
    span = REACH * TOK
    for b in range(2):
        i = jnp.bitwise_xor(core, b)
        prefix = info_ref[1 + i]
        segc = segc_ref[i]
        segr = segr_ref[i]
        leading = segc == segr[:, :1]
        row = lax.broadcasted_iota(jnp.int32, (TOK, TOK), 0)
        col = lax.broadcasted_iota(jnp.int32, (TOK, TOK), 1)
        bias_ref[:, span:] = jnp.where((col <= row) & (segc == segr), 0.0, MASKED)
        rcol = lax.broadcasted_iota(jnp.int32, (TOK, span), 1) - span
        bias_ref[:, :span] = jnp.where((rcol >= -prefix) & leading, 0.0, MASKED)
        keys = kv_ref[b : b + 3, :, :HEAD_DIM].reshape(3 * TOK, HEAD_DIM)
        vals = kv_ref[b : b + 3, :, HEAD_DIM:].reshape(3 * TOK, HEAD_DIM)
        for g in range(group):
            cols = slice(g * HEAD_DIM, (g + 1) * HEAD_DIM)
            q = q_ref[i, :, cols]
            s = lax.dot_general(q, keys, (((1,), (1,)), ((), ())), preferred_element_type=f32)
            s = s * (HEAD_DIM**-0.5 * LOG2E) + bias_ref[...]
            e = jnp.exp2(s - jnp.max(s, axis=1, keepdims=True))
            inv = 1.0 / jnp.sum(e, axis=1, keepdims=True)
            p = (e * inv).astype(bf16)
            o = jnp.dot(p, vals, preferred_element_type=f32)
            rows_ref[:, cols] = o.astype(bf16)
        slots = lax.broadcasted_iota(jnp.int32, (DEV * CAP, TOK), 0)
        pick = jnp.where(slots == slot_ref[i], 1.0, 0.0).astype(bf16)
        packed = jnp.dot(pick, rows_ref[...], preferred_element_type=f32)
        out_ref[:, b] = packed.reshape(DEV, CAP, group * HEAD_DIM).astype(bf16)


def attend(q, cur, prev, info, segc, segr, slot, head):
    width = HEADS // KV_HEADS * HEAD_DIM
    vm = pl.BlockSpec(memory_space=pltpu.VMEM)
    flops = 2 * 8 * TOK * 3 * TOK * HEAD_DIM * 2 + 2 * 2 * DEV * CAP * TOK * width
    return pl.pallas_call(
        functools.partial(attend_kernel, head),
        out_shape=jax.ShapeDtypeStruct((DEV, 2, CAP, width), bf16),
        in_specs=[pl.BlockSpec(memory_space=pltpu.SMEM)] + [vm] * 6,
        out_specs=vm,
        scratch_shapes=[
            pltpu.VMEM((4, TOK, 2 * HEAD_DIM), bf16),
            pltpu.VMEM((TOK, 3 * TOK), f32),
            pltpu.VMEM((TOK, width), bf16),
        ],
        cost_estimate=pl.CostEstimate(
            flops=flops, bytes_accessed=8 * TOK * PART * 2, transcendentals=8 * TOK * 3 * TOK
        ),
        name="attend",
    )(info, q, cur, prev, segc, segr, slot)


def place_kernel(places_ref, first_ref, second_ref, out_ref, pick_ref):
    step = pl.program_id(0)

    @pl.when(step == 0)
    def _():
        rows = lax.broadcasted_iota(jnp.int32, (TOK, DEV * CAP), 0)
        pick_ref[...] = jnp.where(rows == places_ref[...], 1.0, 0.0).astype(bf16)

    for j, ref in enumerate((first_ref, second_ref)):
        got = ref[...].reshape(DEV * CAP, PART)
        out_ref[:, j * PART : (j + 1) * PART] = jnp.dot(
            pick_ref[...], got, preferred_element_type=f32
        ).astype(bf16)


def place(places, first, second):
    spec = pl.BlockSpec((NCHIP, 1, NC * CAP, PART), lambda c: (0, c, 0, 0))
    return pl.pallas_call(
        place_kernel,
        out_shape=jax.ShapeDtypeStruct((TOK, HEADS * HEAD_DIM), bf16),
        grid=(NC,),
        in_specs=[pl.BlockSpec((1, DEV * CAP), lambda c: (0, 0)), spec, spec],
        out_specs=pl.BlockSpec((TOK, 2 * PART), lambda c: (0, c)),
        scratch_shapes=[pltpu.VMEM((TOK, DEV * CAP), bf16)],
        name="place",
    )(places, first, second)


def on_device(tokens, qkv_weight, segments, destination, doc_prefix):
    own = tokens[0]
    core = lax.axis_index("core")
    plane = ("x", "y", "core")
    chips = ("x", "y")

    qw, kw = HEADS * HEAD_DIM // NC, KV_HEADS * HEAD_DIM // NC

    def half(c):
        return jnp.concatenate(
            [
                lax.dynamic_slice_in_dim(qkv_weight, NC * qw + c * kw, kw, 1),
                lax.dynamic_slice_in_dim(qkv_weight, NC * qw + NC * kw + c * kw, kw, 1),
                lax.dynamic_slice_in_dim(qkv_weight, c * qw, qw, 1),
            ],
            axis=1,
        )

    mine = half(core)
    theirs = shift(half(1 - core), "core", NC, 1)
    w = jnp.where(core == 0, jnp.concatenate([mine, theirs]), jnp.concatenate([theirs, mine]))
    other = shift(own, "core", NC, 1)

    wab, wc = w[:, : 2 * PART], w[:, 2 * PART :]
    up, down = shift(wab, "dp", NZ, 1), shift(wab, "dp", NZ, -1)
    up3 = shift(jnp.stack([wab, up, down]), "dp", NZ, 3)
    down3 = shift(jnp.stack([wab, up]), "dp", NZ, -3)
    wz = jnp.concatenate([jnp.stack([wab, up, down]), up3, down3])
    offsets_ab = (0, 1, 7, 3, 4, 2, 5, 6)

    wc = lax.all_gather(wc, chips, axis=0, tiled=True)
    wa = lax.all_gather(wz[:, :, :PART].reshape(NZ * 32, PART), chips, axis=0, tiled=True)
    wb = lax.all_gather(wz[:, :, PART:].reshape(NZ * 32, PART), chips, axis=0, tiled=True)
    wa = wa.reshape(NCHIP, NZ, 32, PART)
    wb = wb.reshape(NCHIP, NZ, 32, PART)

    pieces = [wc]
    right = left = wc
    for _ in range(NZ // 2 - 1):
        right, left = shift(right, "dp", NZ, 1), shift(left, "dp", NZ, -1)
        pieces += [right, left]
    hp = PART // 2
    last = jnp.concatenate(
        [shift(right[:, :hp], "dp", NZ, 1), shift(left[:, hp:], "dp", NZ, -1)], axis=1
    )
    wc = jnp.stack(pieces + [last])
    offsets_c = (0, 1, 7, 2, 6, 3, 5, 4)

    zi = lax.axis_index("dp")
    zs_ab = (zi - jnp.array(offsets_ab, jnp.int32)) % NZ
    zs_c = (zi - jnp.array(offsets_c, jnp.int32)) % NZ

    seg = segments[0]
    prefix = doc_prefix[0, 0]
    target = destination[0]
    owner = target // TOK
    one_hot = (owner[:, None] == jnp.arange(DEV, dtype=jnp.int32)[None, :]).astype(jnp.int32)
    rank = jnp.sum(jnp.cumsum(one_hot, axis=0) * one_hot, axis=1) - 1
    slot = owner * CAP + rank
    place_row = target % TOK
    table = jnp.stack([positions(seg, prefix), seg, slot, jnp.broadcast_to(prefix, seg.shape)])
    tables = jnp.stack([table, shift(table, "core", NC, 1)])
    pos, segs, slots, prefixes = (tables[:, k] for k in range(4))
    frequency = ROPE_BASE ** (
        -2.0 * jnp.arange(HEAD_DIM // 2, dtype=f32) / HEAD_DIM
    )
    angles = pos.astype(f32)[:, :, None] * frequency[None, None, :]
    cosine, sine = jnp.cos(angles), jnp.sin(angles)
    cosine = jnp.concatenate([cosine, cosine], axis=2)
    sine = jnp.concatenate([-sine, sine], axis=2)
    info = jnp.concatenate([core.reshape(1).astype(jnp.int32), prefixes[:, 0]])
    segc, segr, slots = segs[:, :, None], segs[:, None, :], slots[:, None, :]

    send_places = jnp.zeros((DEV * CAP,), jnp.int32).at[slot].set(place_row)
    places = lax.all_to_all(send_places.reshape(DEV, CAP), plane, split_axis=0, concat_axis=0, tiled=True)
    places = places.reshape(1, DEV * CAP)

    cur = project(own, other, wa, zs_ab, cosine, sine, 2)
    prev = lax.ppermute(cur, chips, [(i, i + 1) for i in range(NCHIP - 1)])

    got = [None, None]
    for head, wq, zs in ((1, wc, zs_c), (0, wb, zs_ab)):
        q = project(own, other, wq, zs, cosine, sine, 4)
        packed = attend(q, cur, prev, info, segc, segr, slots, head)
        got[head] = lax.all_to_all(
            packed.reshape(DEV, NC * CAP, PART), plane, split_axis=0, concat_axis=0, tiled=True
        ).reshape(NCHIP, NC, NC * CAP, PART)
    return place(places, got[0], got[1])[None]


def solution(mesh):
    grid = Mesh(mesh.devices.reshape(NZ, NX, NY, NC), ("dp", "x", "y", "core"))
    seq = ("x", "y", "core")
    placed = (P("dp", seq, None), P(("dp", *seq), None), P("dp", seq), P("dp", seq), P("dp", seq))
    return jax.shard_map(
        on_device, mesh=grid, in_specs=placed, out_specs=P("dp", seq, None), check_vma=False
    )
```

```python
import jax
import jax.numpy as jnp
from jax import lax
from jax.experimental import pallas as pl
from jax.experimental.pallas import tpu as pltpu
from jax.sharding import Mesh, PartitionSpec as P


HEADS = 16
KV_HEADS = 4
HEAD_DIM = 128
REACH = 2
ROPE_BASE = 500000.0
MASKED = -1e30
LOG2E = 1.4426950408889634

NZ, NX, NY, NC = 8, 4, 4, 2
NCHIP = NX * NY
TOK = 384
CAP = 24
D = 4096
DEV = NCHIP * NC
PART = 512


bf16 = jnp.bfloat16
f32 = jnp.float32


def shift(x, axis, n, d):
    return lax.ppermute(x, axis, [(i, (i + d) % n) for i in range(n)])


OFFSETS_Z = (0, 1, 7, 3, 4, 2, 5, 6)
OFFSETS_C = (0, 1, 7, 2, 6, 3, 5, 4)


def each(pair, axis, n):
    return [shift(pair[0], axis, n, 1), shift(pair[1], axis, n, -1)]


def positions(segment_ids, prefix_len):
    index_list = jnp.arange(segment_ids.shape[0], dtype=jnp.int32)
    fresh_doc = jnp.concatenate([jnp.ones((1,), jnp.bool_), segment_ids[1:] != segment_ids[:-1]])
    first_row = lax.cummax(jnp.where(fresh_doc, index_list, 0), axis=0)
    leading = segment_ids == segment_ids[0]
    return index_list - first_row + jnp.where(leading, prefix_len, 0)


def assemble_kernel(zs_ref, one_ref, up_ref, down_ref, up3_ref, down3_ref, out_ref):
    pieces = [one_ref[...], up_ref[...], down_ref[...]]
    pieces += [up3_ref[k] for k in range(3)] + [down3_ref[k] for k in range(2)]
    for k, x in enumerate(pieces):
        out_ref[zs_ref[k]] = x


def assemble(zs, *pieces):
    vm = pl.BlockSpec(memory_space=pltpu.VMEM)
    return pl.pallas_call(
        assemble_kernel,
        out_shape=jax.ShapeDtypeStruct((NZ, 32, 2 * PART), bf16),
        in_specs=[pl.BlockSpec(memory_space=pltpu.SMEM)] + [vm] * len(pieces),
        out_specs=vm,
        cost_estimate=SMALL,
        name="assemble",
    )(zs, *pieces)


SMALL = pl.CostEstimate(flops=1 << 20, bytes_accessed=1 << 20, transcendentals=0)
HALF = PART // 2


def finish(acc, rotary, cos_ref, sin_ref, out_ref, b):
    for h in range(HALF // HEAD_DIM):
        x = acc[:, h * HEAD_DIM : (h + 1) * HEAD_DIM]
        if h < rotary:
            x = x * cos_ref[b] + pltpu.roll(x, HEAD_DIM // 2, 1) * sin_ref[b]
        out_ref[b, :, h * HEAD_DIM : (h + 1) * HEAD_DIM] = x.astype(bf16)


def project_kv_kernel(lane_ref, own_ref, other_ref, *refs):
    *w_refs, cos_ref, sin_ref, first_ref, second_ref = refs
    depth = D // NZ
    for n in range(2):
        cols = slice(n * HALF, (n + 1) * HALF)
        for b, ref in enumerate((own_ref, other_ref)):
            acc = None
            for k in range(NZ):
                w = w_refs[k][:, cols] if k < NZ - 1 else w_refs[NZ - 1 + n][...]
                tok = ref[:, pl.ds(pl.multiple_of(lane_ref[k], depth), depth)]
                term = jnp.dot(tok, w, preferred_element_type=f32)
                acc = term if acc is None else acc + term
            finish(acc, 1, cos_ref, sin_ref, (first_ref, second_ref)[n], b)


def project_kv(lanes, *arrays):
    vm = pl.BlockSpec(memory_space=pltpu.VMEM)
    return pl.pallas_call(
        project_kv_kernel,
        out_shape=[jax.ShapeDtypeStruct((2, TOK, HALF), bf16)] * 2,
        in_specs=[pl.BlockSpec(memory_space=pltpu.SMEM)] + [vm] * len(arrays),
        out_specs=[vm, vm],
        cost_estimate=SMALL,
        name="project_kv",
    )(lanes, *arrays)


def project_q_kernel(own_ref, other_ref, w_ref, cos_ref, sin_ref, out_ref):
    depth = D // NZ
    for b, ref in enumerate((own_ref, other_ref)):
        acc = None
        for z in range(NZ):
            w = w_ref[:, z].reshape(depth, HALF)
            term = jnp.dot(ref[:, z * depth : (z + 1) * depth], w, preferred_element_type=f32)
            acc = term if acc is None else acc + term
        finish(acc, 2, cos_ref, sin_ref, out_ref, b)


def project_q(head, own, other, w, cosine, sine):
    tok = pl.BlockSpec((TOK, D), lambda n: (0, 0))
    ang = pl.BlockSpec((2, TOK, HEAD_DIM), lambda n: (0, 0, 0))
    return pl.pallas_call(
        project_q_kernel,
        out_shape=jax.ShapeDtypeStruct((2, TOK, PART), bf16),
        grid=(2,),
        in_specs=[
            tok, tok, pl.BlockSpec((NCHIP, NZ, 32, HALF), lambda n: (0, 0, 0, 2 * head + n)), ang, ang
        ],
        out_specs=pl.BlockSpec((2, TOK, HALF), lambda n: (0, 0, n)),
        cost_estimate=SMALL,
        name="project_q",
    )(own, other, w, cosine, sine)


GROUP = HEADS // KV_HEADS
TILE = 128


def attend_kernel(
    info_ref, q_ref, cur_ref, prev_ref, segc_ref, segr_ref, slot_ref, out_ref, kv_ref, bias_ref, rows_ref
):
    b = pl.program_id(0)
    core = info_ref[0]
    i = jnp.bitwise_xor(core, b)
    span = REACH * TOK

    @pl.when(b == 0)
    def _():
        for n in range(2):
            k = jnp.bitwise_xor(core, n)
            for m, ref in ((n, prev_ref), (2 + n, cur_ref)):
                kv_ref[m, :, : 2 * HEAD_DIM] = ref[k]
                kv_ref[m, :, 2 * HEAD_DIM :] = jnp.ones((TOK, HEAD_DIM), bf16)

    prefix = info_ref[1 + i]
    segc = segc_ref[i]
    segr = segr_ref[i]
    leading = segc == segr[:, :1]
    row = lax.broadcasted_iota(jnp.int32, (TOK, TOK), 0)
    col = lax.broadcasted_iota(jnp.int32, (TOK, TOK), 1)
    bias_ref[:, span:] = jnp.where((col <= row) & (segc == segr), 0.0, MASKED)
    rcol = lax.broadcasted_iota(jnp.int32, (TOK, span), 1) - span
    bias_ref[:, :span] = jnp.where((rcol >= -prefix) & leading, 0.0, MASKED)

    keys = kv_ref[pl.ds(b, 3), :, :HEAD_DIM].reshape(3 * TOK, HEAD_DIM)
    vals = kv_ref[pl.ds(b, 3), :, HEAD_DIM:].reshape(3 * TOK, 2 * HEAD_DIM)
    for r in range(TOK // TILE):
        rows = slice(r * TILE, (r + 1) * TILE)
        n = span + (r + 1) * TILE
        for g in range(GROUP):
            cols = slice(g * HEAD_DIM, (g + 1) * HEAD_DIM)
            s = lax.dot_general(
                q_ref[i, rows, cols], keys[:n], (((1,), (1,)), ((), ())), preferred_element_type=f32
            )
            s = s * (HEAD_DIM**-0.5 * LOG2E) + bias_ref[rows, :n]
            e = jnp.exp2(s - jnp.max(s, axis=1, keepdims=True)).astype(bf16)
            o = jnp.dot(e, vals[:n], preferred_element_type=f32)
            rows_ref[rows, cols] = (o[:, :HEAD_DIM] / o[:, HEAD_DIM:]).astype(bf16)

    slots = lax.broadcasted_iota(jnp.int32, (DEV * CAP, TOK), 0)
    pick = jnp.where(slots == slot_ref[i], 1.0, 0.0).astype(bf16)
    packed = jnp.dot(pick, rows_ref[...], preferred_element_type=f32)
    out_ref[:, 0] = packed.reshape(DEV, CAP, GROUP * HEAD_DIM).astype(bf16)


def attend(q, cur, prev, info, segc, segr, slot):
    width = GROUP * HEAD_DIM

    def whole(x):
        return pl.BlockSpec(x.shape, lambda b, info: (0,) * x.ndim)

    return pl.pallas_call(
        attend_kernel,
        out_shape=jax.ShapeDtypeStruct((DEV, 2, CAP, width), bf16),
        grid_spec=pltpu.PrefetchScalarGridSpec(
            num_scalar_prefetch=1,
            grid=(2,),
            in_specs=[
                whole(q), whole(cur), whole(prev), whole(segc), whole(segr), whole(slot),
            ],
            out_specs=pl.BlockSpec((DEV, 1, CAP, width), lambda b, info: (0, b, 0, 0)),
            scratch_shapes=[
                pltpu.VMEM((4, TOK, 3 * HEAD_DIM), bf16),
                pltpu.VMEM((TOK, 3 * TOK), f32),
                pltpu.VMEM((TOK, width), bf16),
            ],
        ),
        cost_estimate=SMALL,
        name="attend",
    )(info, q, cur, prev, segc, segr, slot)


def place_kernel(places_ref, first_ref, second_ref, out_ref, pick_ref):
    step = pl.program_id(0)

    @pl.when(step == 0)
    def _():
        rows = lax.broadcasted_iota(jnp.int32, (TOK, DEV * CAP), 0)
        pick_ref[...] = jnp.where(rows == places_ref[...], 1.0, 0.0).astype(bf16)

    for j, ref in enumerate((first_ref, second_ref)):
        got = ref[...].reshape(DEV * CAP, PART)
        out_ref[:, j * PART : (j + 1) * PART] = jnp.dot(
            pick_ref[...], got, preferred_element_type=f32
        ).astype(bf16)


def place(places, first, second):
    spec = pl.BlockSpec((NCHIP, 1, NC * CAP, PART), lambda c: (0, c, 0, 0))
    return pl.pallas_call(
        place_kernel,
        out_shape=jax.ShapeDtypeStruct((TOK, HEADS * HEAD_DIM), bf16),
        grid=(NC,),
        in_specs=[pl.BlockSpec((1, DEV * CAP), lambda c: (0, 0)), spec, spec],
        out_specs=pl.BlockSpec((TOK, 2 * PART), lambda c: (0, c)),
        scratch_shapes=[pltpu.VMEM((TOK, DEV * CAP), bf16)],
        cost_estimate=SMALL,
        name="place",
    )(places, first, second)


def on_device(tokens, qkv_weight, segments, destination, doc_prefix):
    own = tokens[0]
    core = lax.axis_index("core")
    plane = ("x", "y", "core")
    chips = ("x", "y")

    qw, kw = HEADS * HEAD_DIM // NC, KV_HEADS * HEAD_DIM // NC

    def kv_half(c):
        first = [NC * qw + c * kw + h * HEAD_DIM + v * NC * kw for h in range(2) for v in range(2)]
        return jnp.concatenate(
            [lax.dynamic_slice_in_dim(qkv_weight, f, HEAD_DIM, 1) for f in first], axis=1
        )

    def q_half(c):
        return lax.dynamic_slice_in_dim(qkv_weight, c * qw, qw, 1)

    def by_core(x, y):
        return jnp.where(core == 0, jnp.concatenate([x, y]), jnp.concatenate([y, x]))

    def swapped(half):
        return by_core(half(core), shift(half(1 - core), "core", NC, 1))

    w = swapped(lambda c: jnp.concatenate([kv_half(c), q_half(c)], axis=1))
    wc, wab = w[:, :PART], w[:, PART:]
    other = shift(own, "core", NC, 1)

    seg = segments[0]
    prefix = doc_prefix[0, 0]
    target = destination[0]
    owner = target // TOK
    one_hot = (owner[:, None] == jnp.arange(DEV, dtype=jnp.int32)[None, :]).astype(jnp.int32)
    rank = jnp.sum(jnp.cumsum(one_hot, axis=0) * one_hot, axis=1) - 1
    slot = owner * CAP + rank
    table = jnp.stack(
        [positions(seg, prefix), seg, slot, target % TOK, jnp.broadcast_to(prefix, seg.shape)]
    )
    tables = jnp.stack([table, shift(table, "core", NC, 1)])
    pos, segs, slots, rows, prefixes = (tables[:, k] for k in range(5))
    hit = slots[:, None, :] == jnp.arange(DEV * CAP, dtype=jnp.int32)[None, :, None]
    send = jnp.sum(jnp.where(hit, rows[:, None, :], 0), axis=2).reshape(2, NCHIP, NC, CAP)
    send = lax.dynamic_index_in_dim(send, core, 2, keepdims=False)
    send = jnp.where(core == 0, send, send[::-1]).transpose(1, 0, 2).reshape(NCHIP, NC * CAP)
    send = jnp.concatenate([send // 16, send % 16], axis=1).astype(bf16)
    send = jnp.pad(send[:, None, :], ((0, 0), (0, 15), (0, PART - 2 * NC * CAP)))
    frequency = ROPE_BASE ** (
        -2.0 * jnp.arange(HEAD_DIM // 2, dtype=f32) / HEAD_DIM
    )
    angles = pos.astype(f32)[:, :, None] * frequency[None, None, :]
    cosine, sine = jnp.cos(angles), jnp.sin(angles)
    cosine = jnp.concatenate([cosine, cosine], axis=2)
    sine = jnp.concatenate([-sine, sine], axis=2)
    info = jnp.concatenate([core.reshape(1).astype(jnp.int32), prefixes[:, 0]])
    segc, segr, slots = segs[:, :, None], segs[:, None, :], slots[:, None, :]

    zi = lax.axis_index("dp").astype(jnp.int32)
    z_ab = (zi - jnp.array(OFFSETS_Z, jnp.int32)) % NZ
    lanes = (zi - jnp.array(OFFSETS_C, jnp.int32)) % NZ * (D // NZ)

    tie = lax.optimization_barrier
    up, down = shift(wab, "dp", NZ, 1), shift(wab, "dp", NZ, -1)
    up, down, wc = tie((up, down, wc))
    up3 = shift(jnp.stack([wab, up, down]), "dp", NZ, 3)
    down3 = shift(jnp.stack([wab, up]), "dp", NZ, -3)
    wz = assemble(z_ab, wab, up, down, up3, down3)
    wq = lax.all_gather(wz.reshape(NZ * 32, 2 * PART), chips, axis=0, tiled=True)

    first = jnp.concatenate([jnp.broadcast_to(wc[None], (NCHIP, *wc.shape)), send], axis=1)
    first = lax.all_to_all(first, chips, split_axis=0, concat_axis=0, tiled=True)
    c0 = first[:, :32].reshape(D // NZ, PART)
    places = first[:, 32, : 2 * NC * CAP].astype(jnp.int32)
    places = (places[:, : NC * CAP] * 16 + places[:, NC * CAP :]).reshape(1, DEV * CAP)
    c1 = each([c0, c0], "dp", NZ)
    c2 = each(c1, "dp", NZ)
    c3 = each(c2, "dp", NZ)
    c4 = each([c3[0][:, :HALF], c3[1][:, HALF:]], "dp", NZ)
    cur = project_kv(lanes, own, other, c0, *c1, *c2, *c3, *c4, cosine, sine)
    onward = [(i, i + 1) for i in range(NCHIP - 1)]
    prev = []
    for h in range(2):
        prev.append(lax.ppermute(cur[h], chips, onward))
    wq = wq.reshape(NCHIP, NZ, 32, 2 * PART)

    got = []
    for head in range(2):
        q = project_q(head, own, other, wq, cosine, sine)
        packed = attend(q, cur[head], prev[head], info, segc, segr, slots)
        got.append(
            lax.all_to_all(
                packed.reshape(DEV, NC * CAP, PART), plane, split_axis=0, concat_axis=0, tiled=True
            ).reshape(NCHIP, NC, NC * CAP, PART)
        )
    return place(places, got[0], got[1])[None]


def solution(mesh):
    grid = Mesh(mesh.devices.reshape(NZ, NX, NY, NC), ("dp", "x", "y", "core"))
    seq = ("x", "y", "core")
    placed = (P("dp", seq, None), P(("dp", *seq), None), P("dp", seq), P("dp", seq), P("dp", seq))

    return jax.shard_map(
        on_device, mesh=grid, in_specs=placed, out_specs=P("dp", seq, None), check_vma=False
    )
```

```python
import jax
import jax.numpy as jnp
from jax import lax
from jax.experimental import pallas as pl
from jax.experimental.pallas import tpu as pltpu
from jax.sharding import Mesh, PartitionSpec as P


HEADS = 16
KV_HEADS = 4
HEAD_DIM = 128
REACH = 2
ROPE_BASE = 500000.0
MASKED = -1e30
LOG2E = 1.4426950408889634

NZ, NX, NY, NC = 8, 4, 4, 2
NCHIP = NX * NY
TOK = 384
CAP = 24
D = 4096
DEV = NCHIP * NC
PART = 512


bf16 = jnp.bfloat16
f32 = jnp.float32


def shift(x, axis, n, d):
    return lax.ppermute(x, axis, [(i, (i + d) % n) for i in range(n)])


OFFSETS_Z = (0, 1, 7, 4, 2, 3, 6, 5)
OFFSETS_C = (0, 1, 7, 2, 6, 3, 5, 4)


def each(pair, axis, n):
    return [shift(pair[0], axis, n, 1), shift(pair[1], axis, n, -1)]


def positions(segment_ids, prefix_len):
    index_list = jnp.arange(segment_ids.shape[0], dtype=jnp.int32)
    fresh_doc = jnp.concatenate([jnp.ones((1,), jnp.bool_), segment_ids[1:] != segment_ids[:-1]])
    first_row = lax.cummax(jnp.where(fresh_doc, index_list, 0), axis=0)
    leading = segment_ids == segment_ids[0]
    return index_list - first_row + jnp.where(leading, prefix_len, 0)


def split_kernel(core_ref, w_ref, mine_ref, theirs_ref):
    qw, kw = HEADS * HEAD_DIM // NC, KV_HEADS * HEAD_DIM // NC
    for ref, c in ((mine_ref, core_ref[0]), (theirs_ref, 1 - core_ref[0])):
        for h in range(2):
            for v in range(2):
                first = NC * qw + h * HEAD_DIM + v * NC * kw
                at = (2 * h + v) * HEAD_DIM
                ref[:, at : at + HEAD_DIM] = w_ref[
                    :, pl.ds(pl.multiple_of(first + c * kw, HEAD_DIM), HEAD_DIM)
                ]
        ref[:, PART:] = w_ref[:, pl.ds(pl.multiple_of(c * qw, HEAD_DIM), qw)]


def merge_kernel(core_ref, mine_ref, theirs_ref, c_ref, ab_ref):
    rows = mine_ref.shape[0]
    for ref, c in ((mine_ref, core_ref[0]), (theirs_ref, 1 - core_ref[0])):
        at = pl.ds(pl.multiple_of(c * rows, rows), rows)
        for p in range(NCHIP):
            c_ref[p, at, :] = ref[:, :PART]
        ab_ref[at, :] = ref[:, PART:]


def small_call(kernel, shapes, scalars, *arrays):
    vm = pl.BlockSpec(memory_space=pltpu.VMEM)
    return pl.pallas_call(
        kernel,
        out_shape=[jax.ShapeDtypeStruct(x, bf16) for x in shapes],
        in_specs=[pl.BlockSpec(memory_space=pltpu.SMEM)] + [vm] * len(arrays),
        out_specs=[vm] * len(shapes),
        cost_estimate=SMALL,
    )(scalars, *arrays)


def split(core_id, w):
    return small_call(split_kernel, [(16, 3 * PART)] * 2, core_id, w)


def merge(core_id, mine, theirs):
    return small_call(merge_kernel, [(NCHIP, 32, PART), (32, 2 * PART)], core_id, mine, theirs)


def assemble_kernel(zs_ref, one_ref, up_ref, down_ref, far_ref, up2_ref, down2_ref, out_ref):
    pieces = [one_ref[...], up_ref[...], down_ref[...], far_ref[...]]
    pieces += [r[k] for r in (up2_ref, down2_ref) for k in range(2)]
    for k, x in enumerate(pieces):
        out_ref[zs_ref[k]] = x


def assemble(zs, *pieces):
    vm = pl.BlockSpec(memory_space=pltpu.VMEM)
    return pl.pallas_call(
        assemble_kernel,
        out_shape=jax.ShapeDtypeStruct((NZ, 32, 2 * PART), bf16),
        in_specs=[pl.BlockSpec(memory_space=pltpu.SMEM)] + [vm] * len(pieces),
        out_specs=vm,
        cost_estimate=SMALL,
        name="assemble",
    )(zs, *pieces)


SMALL = pl.CostEstimate(flops=1 << 20, bytes_accessed=1 << 20, transcendentals=0)
HALF = PART // 2


def finish(acc, rotary, cos_ref, sin_ref, out_ref, b):
    for h in range(HALF // HEAD_DIM):
        x = acc[:, h * HEAD_DIM : (h + 1) * HEAD_DIM]
        if h < rotary:
            x = x * cos_ref[b] + pltpu.roll(x, HEAD_DIM // 2, 1) * sin_ref[b]
        out_ref[b, :, h * HEAD_DIM : (h + 1) * HEAD_DIM] = x.astype(bf16)


def project_kv_kernel(lane_ref, own_ref, other_ref, *refs):
    *w_refs, cos_ref, sin_ref, first_ref, second_ref = refs
    depth = D // NZ
    for n in range(2):
        cols = slice(n * HALF, (n + 1) * HALF)
        for b, ref in enumerate((own_ref, other_ref)):
            acc = None
            for k in range(NZ):
                w = w_refs[k][:, cols] if k < NZ - 1 else w_refs[NZ - 1 + n][...]
                tok = ref[:, pl.ds(pl.multiple_of(lane_ref[k], depth), depth)]
                term = jnp.dot(tok, w, preferred_element_type=f32)
                acc = term if acc is None else acc + term
            finish(acc, 1, cos_ref, sin_ref, (first_ref, second_ref)[n], b)


def project_kv(lanes, *arrays):
    vm = pl.BlockSpec(memory_space=pltpu.VMEM)
    return pl.pallas_call(
        project_kv_kernel,
        out_shape=[jax.ShapeDtypeStruct((2, TOK, HALF), bf16)] * 2,
        in_specs=[pl.BlockSpec(memory_space=pltpu.SMEM)] + [vm] * len(arrays),
        out_specs=[vm, vm],
        cost_estimate=SMALL,
        name="project_kv",
    )(lanes, *arrays)


def project_q_kernel(own_ref, other_ref, w_ref, cos_ref, sin_ref, out_ref):
    depth = D // NZ
    for b, ref in enumerate((own_ref, other_ref)):
        acc = None
        for z in range(NZ):
            w = w_ref[:, z].reshape(depth, HALF)
            term = jnp.dot(ref[:, z * depth : (z + 1) * depth], w, preferred_element_type=f32)
            acc = term if acc is None else acc + term
        finish(acc, 2, cos_ref, sin_ref, out_ref, b)


def project_q(head, own, other, w, cosine, sine):
    tok = pl.BlockSpec((TOK, D), lambda n: (0, 0))
    ang = pl.BlockSpec((2, TOK, HEAD_DIM), lambda n: (0, 0, 0))
    return pl.pallas_call(
        project_q_kernel,
        out_shape=jax.ShapeDtypeStruct((2, TOK, PART), bf16),
        grid=(2,),
        in_specs=[
            tok, tok, pl.BlockSpec((NCHIP, NZ, 32, HALF), lambda n: (0, 0, 0, 2 * head + n)), ang, ang
        ],
        out_specs=pl.BlockSpec((2, TOK, HALF), lambda n: (0, 0, n)),
        cost_estimate=SMALL,
        name="project_q",
    )(own, other, w, cosine, sine)


GROUP = HEADS // KV_HEADS
TILE = 128


def attend_kernel(
    info_ref, q_ref, cur_ref, prev_ref, segc_ref, segr_ref, slot_ref, out_ref, kv_ref, bias_ref, rows_ref
):
    b = pl.program_id(0)
    core = info_ref[0]
    i = jnp.bitwise_xor(core, b)
    span = REACH * TOK

    @pl.when(b == 0)
    def _():
        for n in range(2):
            k = jnp.bitwise_xor(core, n)
            for m, ref in ((n, prev_ref), (2 + n, cur_ref)):
                kv_ref[m, :, : 2 * HEAD_DIM] = ref[k]
                kv_ref[m, :, 2 * HEAD_DIM :] = jnp.ones((TOK, HEAD_DIM), bf16)

    prefix = info_ref[1 + i]
    segc = segc_ref[i]
    segr = segr_ref[i]
    leading = segc == segr[:, :1]
    row = lax.broadcasted_iota(jnp.int32, (TOK, TOK), 0)
    col = lax.broadcasted_iota(jnp.int32, (TOK, TOK), 1)
    bias_ref[:, span:] = jnp.where((col <= row) & (segc == segr), 0.0, MASKED)
    rcol = lax.broadcasted_iota(jnp.int32, (TOK, span), 1) - span
    bias_ref[:, :span] = jnp.where((rcol >= -prefix) & leading, 0.0, MASKED)

    keys = kv_ref[pl.ds(b, 3), :, :HEAD_DIM].reshape(3 * TOK, HEAD_DIM)
    vals = kv_ref[pl.ds(b, 3), :, HEAD_DIM:].reshape(3 * TOK, 2 * HEAD_DIM)
    for r in range(TOK // TILE):
        rows = slice(r * TILE, (r + 1) * TILE)
        n = span + (r + 1) * TILE
        for g in range(GROUP):
            cols = slice(g * HEAD_DIM, (g + 1) * HEAD_DIM)
            s = lax.dot_general(
                q_ref[i, rows, cols], keys[:n], (((1,), (1,)), ((), ())), preferred_element_type=f32
            )
            s = s * (HEAD_DIM**-0.5 * LOG2E) + bias_ref[rows, :n]
            e = jnp.exp2(s - jnp.max(s, axis=1, keepdims=True)).astype(bf16)
            o = jnp.dot(e, vals[:n], preferred_element_type=f32)
            rows_ref[rows, cols] = (o[:, :HEAD_DIM] / o[:, HEAD_DIM:]).astype(bf16)

    slots = lax.broadcasted_iota(jnp.int32, (DEV * CAP, TOK), 0)
    pick = jnp.where(slots == slot_ref[i], 1.0, 0.0).astype(bf16)
    packed = jnp.dot(pick, rows_ref[...], preferred_element_type=f32)
    out_ref[:, 0] = packed.reshape(DEV, CAP, GROUP * HEAD_DIM).astype(bf16)


def attend(q, cur, prev, info, segc, segr, slot):
    width = GROUP * HEAD_DIM

    def whole(x):
        return pl.BlockSpec(x.shape, lambda b, info: (0,) * x.ndim)

    return pl.pallas_call(
        attend_kernel,
        out_shape=jax.ShapeDtypeStruct((DEV, 2, CAP, width), bf16),
        grid_spec=pltpu.PrefetchScalarGridSpec(
            num_scalar_prefetch=1,
            grid=(2,),
            in_specs=[
                whole(q), whole(cur), whole(prev), whole(segc), whole(segr), whole(slot),
            ],
            out_specs=pl.BlockSpec((DEV, 1, CAP, width), lambda b, info: (0, b, 0, 0)),
            scratch_shapes=[
                pltpu.VMEM((4, TOK, 3 * HEAD_DIM), bf16),
                pltpu.VMEM((TOK, 3 * TOK), f32),
                pltpu.VMEM((TOK, width), bf16),
            ],
        ),
        cost_estimate=SMALL,
        name="attend",
    )(info, q, cur, prev, segc, segr, slot)


def place_kernel(places_ref, got_ref, *refs):
    out_ref, pick_ref = refs[-2:]

    @pl.when(pl.program_id(0) == 0)
    def _():
        rows = lax.broadcasted_iota(jnp.int32, (TOK, DEV * CAP), 0)
        pick_ref[...] = jnp.where(rows == places_ref[...], 1.0, 0.0).astype(bf16)

    out_ref[...] = jnp.dot(
        pick_ref[...], got_ref[...].reshape(DEV * CAP, PART), preferred_element_type=f32
    ).astype(bf16)


def place(places, got, head, whole):
    return pl.pallas_call(
        place_kernel,
        out_shape=jax.ShapeDtypeStruct((TOK, HEADS * HEAD_DIM), bf16),
        grid=(NC,),
        in_specs=[
            pl.BlockSpec((1, DEV * CAP), lambda c: (0, 0)),
            pl.BlockSpec((NCHIP, 1, NC * CAP, PART), lambda c: (0, c, 0, 0)),
        ]
        + [pl.BlockSpec(memory_space=pl.ANY)] * len(whole),
        out_specs=pl.BlockSpec((TOK, PART), lambda c: (0, 2 * c + head)),
        scratch_shapes=[pltpu.VMEM((TOK, DEV * CAP), bf16)],
        input_output_aliases={2: 0} if whole else {},
        cost_estimate=SMALL,
        name="place",
    )(places, got, *whole)


def on_device(tokens, qkv_weight, segments, destination, doc_prefix):
    own = tokens[0]
    core = lax.axis_index("core")
    plane = ("x", "y", "core")
    chips = ("x", "y")

    core_id = core.reshape(1).astype(jnp.int32)
    mine, theirs = split(core_id, qkv_weight)
    wc, wab = merge(core_id, mine, shift(theirs, "core", NC, 1))
    other = shift(own, "core", NC, 1)

    seg = segments[0]
    prefix = doc_prefix[0, 0]
    target = destination[0]
    owner = target // TOK
    one_hot = (owner[:, None] == jnp.arange(DEV, dtype=jnp.int32)[None, :]).astype(jnp.int32)
    rank = jnp.sum(jnp.cumsum(one_hot, axis=0) * one_hot, axis=1) - 1
    slot = owner * CAP + rank
    table = jnp.stack([positions(seg, prefix), seg, slot, jnp.broadcast_to(prefix, seg.shape)])
    tables = jnp.stack([table, shift(table, "core", NC, 1)])
    pos, segs, slots, prefixes = (tables[:, k] for k in range(4))
    hit = slot[None, :] == jnp.arange(DEV * CAP, dtype=jnp.int32)[:, None]
    send_places = jnp.sum(jnp.where(hit, (target % TOK)[None, :], 0), axis=1)
    frequency = ROPE_BASE ** (
        -2.0 * jnp.arange(HEAD_DIM // 2, dtype=f32) / HEAD_DIM
    )
    angles = pos.astype(f32)[:, :, None] * frequency[None, None, :]
    cosine, sine = jnp.cos(angles), jnp.sin(angles)
    cosine = jnp.concatenate([cosine, cosine], axis=2)
    sine = jnp.concatenate([-sine, sine], axis=2)
    info = jnp.concatenate([core.reshape(1).astype(jnp.int32), prefixes[:, 0]])
    segc, segr, slots = segs[:, :, None], segs[:, None, :], slots[:, None, :]

    zi = lax.axis_index("dp").astype(jnp.int32)
    z_ab = (zi - jnp.array(OFFSETS_Z, jnp.int32)) % NZ
    lanes = (zi - jnp.array(OFFSETS_C, jnp.int32)) % NZ * (D // NZ)

    tie = lax.optimization_barrier
    c0 = lax.all_to_all(wc, chips, split_axis=0, concat_axis=0, tiled=True)
    c0 = c0.reshape(D // NZ, PART)
    up = shift(wab, "dp", NZ, 1)
    down = shift(wab, "dp", NZ, -1)
    far = shift(wab, "dp", NZ, 4)
    up2 = shift(jnp.stack([wab, up]), "dp", NZ, 2)
    down2 = shift(jnp.stack([wab, down]), "dp", NZ, -2)
    wz = assemble(z_ab, wab, up, down, far, up2, down2)
    wq = lax.all_gather(wz.reshape(NZ * 32, 2 * PART), chips, axis=0, tiled=True)

    c1 = [shift(c0, "dp", NZ, 1)]
    c1.append(shift(c0, "dp", NZ, -1))
    places = lax.all_to_all(
        send_places.reshape(DEV, CAP), plane, split_axis=0, concat_axis=0, tiled=True
    ).reshape(1, DEV * CAP)
    c2 = each(c1, "dp", NZ)
    c2, places = tie((c2, places))
    c3 = each(c2, "dp", NZ)
    c4 = each([c3[0][:, :HALF], c3[1][:, HALF:]], "dp", NZ)
    cur = project_kv(lanes, own, other, c0, *c1, *c2, *c3, *c4, cosine, sine)
    onward = [(i, i + 1) for i in range(NCHIP - 1)]
    prev = []
    for h in range(2):
        prev.append(lax.ppermute(cur[h], chips, onward))
    wq = wq.reshape(NCHIP, NZ, 32, 2 * PART)

    whole = []
    for head in range(2):
        q = project_q(head, own, other, wq, cosine, sine)
        packed = attend(q, cur[head], prev[head], info, segc, segr, slots)
        got = lax.all_to_all(
            packed.reshape(DEV, NC * CAP, PART), plane, split_axis=0, concat_axis=0, tiled=True
        ).reshape(NCHIP, NC, NC * CAP, PART)
        whole = [place(places, got, head, whole)]
    return whole[0][None]


def solution(mesh):
    grid = Mesh(mesh.devices.reshape(NZ, NX, NY, NC), ("dp", "x", "y", "core"))
    seq = ("x", "y", "core")
    placed = (P("dp", seq, None), P(("dp", *seq), None), P("dp", seq), P("dp", seq), P("dp", seq))

    return jax.shard_map(
        on_device, mesh=grid, in_specs=placed, out_specs=P("dp", seq, None), check_vma=False
    )
```

```python
import jax
import jax.numpy as jnp
from jax import lax
from jax.experimental import pallas as pl
from jax.experimental.pallas import tpu as pltpu
from jax.sharding import Mesh, PartitionSpec as P


HEADS = 16
KV_HEADS = 4
HEAD_DIM = 128
REACH = 2
ROPE_BASE = 500000.0
MASKED = -1e30
LOG2E = 1.4426950408889634

NZ, NX, NY, NC = 8, 4, 4, 2
NCHIP = NX * NY
TOK = 384
CAP = 24
D = 4096
DEV = NCHIP * NC
PART = 512


bf16 = jnp.bfloat16
f32 = jnp.float32


def shift(x, axis, n, d):
    return lax.ppermute(x, axis, [(i, (i + d) % n) for i in range(n)])


OFFSETS_Z = (0, 1, 7, 4, 2, 3, 6, 5)
OFFSETS_C = (0, 1, 7, 2, 6, 3, 5, 4)


def each(pair, axis, n):
    return [shift(pair[0], axis, n, 1), shift(pair[1], axis, n, -1)]


def positions(segment_ids, prefix_len):
    index_list = jnp.arange(segment_ids.shape[0], dtype=jnp.int32)
    fresh_doc = jnp.concatenate([jnp.ones((1,), jnp.bool_), segment_ids[1:] != segment_ids[:-1]])
    first_row = lax.cummax(jnp.where(fresh_doc, index_list, 0), axis=0)
    leading = segment_ids == segment_ids[0]
    return index_list - first_row + jnp.where(leading, prefix_len, 0)


def split_kernel(core_ref, w_ref, mine_ref, theirs_ref):
    qw, kw = HEADS * HEAD_DIM // NC, KV_HEADS * HEAD_DIM // NC
    for ref, c in ((mine_ref, core_ref[0]), (theirs_ref, 1 - core_ref[0])):
        for h in range(2):
            for v in range(2):
                first = NC * qw + h * HEAD_DIM + v * NC * kw
                at = (2 * h + v) * HEAD_DIM
                ref[:, at : at + HEAD_DIM] = w_ref[
                    :, pl.ds(pl.multiple_of(first + c * kw, HEAD_DIM), HEAD_DIM)
                ]
        ref[:, PART:] = w_ref[:, pl.ds(pl.multiple_of(c * qw, HEAD_DIM), qw)]


def merge_kernel(core_ref, mine_ref, theirs_ref, c_ref, ab_ref):
    rows = mine_ref.shape[0]
    for ref, c in ((mine_ref, core_ref[0]), (theirs_ref, 1 - core_ref[0])):
        at = pl.ds(pl.multiple_of(c * rows, rows), rows)
        for p in range(NCHIP):
            c_ref[p, at, :] = ref[:, :PART]
        ab_ref[at, :] = ref[:, PART:]


def small_call(kernel, shapes, scalars, *arrays):
    vm = pl.BlockSpec(memory_space=pltpu.VMEM)
    return pl.pallas_call(
        kernel,
        out_shape=[jax.ShapeDtypeStruct(x, bf16) for x in shapes],
        in_specs=[pl.BlockSpec(memory_space=pltpu.SMEM)] + [vm] * len(arrays),
        out_specs=[vm] * len(shapes),
        cost_estimate=SMALL,
    )(scalars, *arrays)


def split(core_id, w):
    return small_call(split_kernel, [(16, 3 * PART)] * 2, core_id, w)


def merge(core_id, mine, theirs):
    return small_call(merge_kernel, [(NCHIP, 32, PART), (32, 2 * PART)], core_id, mine, theirs)


def assemble_kernel(zs_ref, one_ref, up_ref, down_ref, far_ref, up2_ref, down2_ref, out_ref):
    pieces = [one_ref[...], up_ref[...], down_ref[...], far_ref[...]]
    pieces += [r[k] for r in (up2_ref, down2_ref) for k in range(2)]
    for k, x in enumerate(pieces):
        out_ref[zs_ref[k]] = x


def assemble(zs, *pieces):
    vm = pl.BlockSpec(memory_space=pltpu.VMEM)
    return pl.pallas_call(
        assemble_kernel,
        out_shape=jax.ShapeDtypeStruct((NZ, 32, 2 * PART), bf16),
        in_specs=[pl.BlockSpec(memory_space=pltpu.SMEM)] + [vm] * len(pieces),
        out_specs=vm,
        cost_estimate=SMALL,
        name="assemble",
    )(zs, *pieces)


SMALL = pl.CostEstimate(flops=1 << 20, bytes_accessed=1 << 20, transcendentals=0)
HALF = PART // 2


def finish(acc, rotary, cos_ref, sin_ref, out_ref, b):
    for h in range(HALF // HEAD_DIM):
        x = acc[:, h * HEAD_DIM : (h + 1) * HEAD_DIM]
        if h < rotary:
            x = x * cos_ref[b] + pltpu.roll(x, HEAD_DIM // 2, 1) * sin_ref[b]
        out_ref[b, :, h * HEAD_DIM : (h + 1) * HEAD_DIM] = x.astype(bf16)


def project_kv_kernel(lane_ref, own_ref, other_ref, *refs):
    *w_refs, cos_ref, sin_ref, first_ref, second_ref = refs
    depth = D // NZ
    for n in range(2):
        cols = slice(n * HALF, (n + 1) * HALF)
        acc = None
        for k in range(NZ):
            w = w_refs[k][:, cols] if k < NZ - 1 else w_refs[NZ - 1 + n][...]
            at = pl.ds(pl.multiple_of(lane_ref[k], depth), depth)
            tok = jnp.concatenate([own_ref[:, at], other_ref[:, at]])
            term = jnp.dot(tok, w, preferred_element_type=f32)
            acc = term if acc is None else acc + term
        for b in range(2):
            rows = acc[b * TOK : (b + 1) * TOK]
            finish(rows, 1, cos_ref, sin_ref, (first_ref, second_ref)[n], b)


def project_kv(lanes, *arrays):
    vm = pl.BlockSpec(memory_space=pltpu.VMEM)
    return pl.pallas_call(
        project_kv_kernel,
        out_shape=[jax.ShapeDtypeStruct((2, TOK, HALF), bf16)] * 2,
        in_specs=[pl.BlockSpec(memory_space=pltpu.SMEM)] + [vm] * len(arrays),
        out_specs=[vm, vm],
        cost_estimate=SMALL,
        name="project_kv",
    )(lanes, *arrays)


def project_q_kernel(own_ref, other_ref, w_ref, cos_ref, sin_ref, out_ref):
    depth = D // NZ
    acc = None
    for z in range(NZ):
        w = w_ref[:, z].reshape(depth, HALF)
        at = slice(z * depth, (z + 1) * depth)
        tok = jnp.concatenate([own_ref[:, at], other_ref[:, at]])
        term = jnp.dot(tok, w, preferred_element_type=f32)
        acc = term if acc is None else acc + term
    for b in range(2):
        finish(acc[b * TOK : (b + 1) * TOK], 2, cos_ref, sin_ref, out_ref, b)


def project_q(head, own, other, w, cosine, sine):
    tok = pl.BlockSpec((TOK, D), lambda n: (0, 0))
    ang = pl.BlockSpec((2, TOK, HEAD_DIM), lambda n: (0, 0, 0))
    return pl.pallas_call(
        project_q_kernel,
        out_shape=jax.ShapeDtypeStruct((2, TOK, PART), bf16),
        grid=(2,),
        in_specs=[
            tok, tok, pl.BlockSpec((NCHIP, NZ, 32, HALF), lambda n: (0, 0, 0, 2 * head + n)), ang, ang
        ],
        out_specs=pl.BlockSpec((2, TOK, HALF), lambda n: (0, 0, n)),
        cost_estimate=SMALL,
        name="project_q",
    )(own, other, w, cosine, sine)


GROUP = HEADS // KV_HEADS
TILE = 128


def attend_kernel(
    info_ref, q_ref, cur_ref, prev_ref, segc_ref, segr_ref, slot_ref, out_ref, kv_ref, bias_ref, rows_ref
):
    b = pl.program_id(0)
    core = info_ref[0]
    i = jnp.bitwise_xor(core, b)
    span = REACH * TOK

    @pl.when(b == 0)
    def _():
        for n in range(2):
            k = jnp.bitwise_xor(core, n)
            for m, ref in ((n, prev_ref), (2 + n, cur_ref)):
                kv_ref[m, :, : 2 * HEAD_DIM] = ref[k]
                kv_ref[m, :, 2 * HEAD_DIM :] = jnp.ones((TOK, HEAD_DIM), bf16)

    prefix = info_ref[1 + i]
    segc = segc_ref[i]
    segr = segr_ref[i]
    leading = segc == segr[:, :1]
    row = lax.broadcasted_iota(jnp.int32, (TOK, TOK), 0)
    col = lax.broadcasted_iota(jnp.int32, (TOK, TOK), 1)
    bias_ref[:, span:] = jnp.where((col <= row) & (segc == segr), 0.0, MASKED)
    rcol = lax.broadcasted_iota(jnp.int32, (TOK, span), 1) - span
    bias_ref[:, :span] = jnp.where((rcol >= -prefix) & leading, 0.0, MASKED)

    keys = kv_ref[pl.ds(b, 3), :, :HEAD_DIM].reshape(3 * TOK, HEAD_DIM)
    vals = kv_ref[pl.ds(b, 3), :, HEAD_DIM:].reshape(3 * TOK, 2 * HEAD_DIM)
    for r in range(TOK // TILE):
        rows = slice(r * TILE, (r + 1) * TILE)
        n = span + (r + 1) * TILE
        for g in range(GROUP):
            cols = slice(g * HEAD_DIM, (g + 1) * HEAD_DIM)
            s = lax.dot_general(
                q_ref[i, rows, cols], keys[:n], (((1,), (1,)), ((), ())), preferred_element_type=f32
            )
            s = s * (HEAD_DIM**-0.5 * LOG2E) + bias_ref[rows, :n]
            e = jnp.exp2(s - jnp.max(s, axis=1, keepdims=True)).astype(bf16)
            o = jnp.dot(e, vals[:n], preferred_element_type=f32)
            rows_ref[rows, cols] = (o[:, :HEAD_DIM] / o[:, HEAD_DIM:]).astype(bf16)

    slots = lax.broadcasted_iota(jnp.int32, (DEV * CAP, TOK), 0)
    pick = jnp.where(slots == slot_ref[i], 1.0, 0.0).astype(bf16)
    packed = jnp.dot(pick, rows_ref[...], preferred_element_type=f32)
    out_ref[:, 0] = packed.reshape(DEV, CAP, GROUP * HEAD_DIM).astype(bf16)


def attend(q, cur, prev, info, segc, segr, slot):
    width = GROUP * HEAD_DIM

    def whole(x):
        return pl.BlockSpec(x.shape, lambda b, info: (0,) * x.ndim)

    return pl.pallas_call(
        attend_kernel,
        out_shape=jax.ShapeDtypeStruct((DEV, 2, CAP, width), bf16),
        grid_spec=pltpu.PrefetchScalarGridSpec(
            num_scalar_prefetch=1,
            grid=(2,),
            in_specs=[
                whole(q), whole(cur), whole(prev), whole(segc), whole(segr), whole(slot),
            ],
            out_specs=pl.BlockSpec((DEV, 1, CAP, width), lambda b, info: (0, b, 0, 0)),
            scratch_shapes=[
                pltpu.VMEM((4, TOK, 3 * HEAD_DIM), bf16),
                pltpu.VMEM((TOK, 3 * TOK), f32),
                pltpu.VMEM((TOK, width), bf16),
            ],
        ),
        cost_estimate=SMALL,
        name="attend",
    )(info, q, cur, prev, segc, segr, slot)


def place_kernel(places_ref, got_ref, *refs):
    out_ref, pick_ref = refs[-2:]

    @pl.when(pl.program_id(0) == 0)
    def _():
        rows = lax.broadcasted_iota(jnp.int32, (TOK, DEV * CAP), 0)
        pick_ref[...] = jnp.where(rows == places_ref[...], 1.0, 0.0).astype(bf16)

    out_ref[...] = jnp.dot(
        pick_ref[...], got_ref[...].reshape(DEV * CAP, PART), preferred_element_type=f32
    ).astype(bf16)


def place(places, got, head, whole):
    return pl.pallas_call(
        place_kernel,
        out_shape=jax.ShapeDtypeStruct((TOK, HEADS * HEAD_DIM), bf16),
        grid=(NC,),
        in_specs=[
            pl.BlockSpec((1, DEV * CAP), lambda c: (0, 0)),
            pl.BlockSpec((NCHIP, 1, NC * CAP, PART), lambda c: (0, c, 0, 0)),
        ]
        + [pl.BlockSpec(memory_space=pl.ANY)] * len(whole),
        out_specs=pl.BlockSpec((TOK, PART), lambda c: (0, 2 * c + head)),
        scratch_shapes=[pltpu.VMEM((TOK, DEV * CAP), bf16)],
        input_output_aliases={2: 0} if whole else {},
        cost_estimate=SMALL,
        name="place",
    )(places, got, *whole)


def on_device(tokens, qkv_weight, segments, destination, doc_prefix):
    own = tokens[0]
    core = lax.axis_index("core")
    plane = ("x", "y", "core")
    chips = ("x", "y")

    core_id = core.reshape(1).astype(jnp.int32)
    mine, theirs = split(core_id, qkv_weight)
    wc, wab = merge(core_id, mine, shift(theirs, "core", NC, 1))
    other = shift(own, "core", NC, 1)

    seg = segments[0]
    prefix = doc_prefix[0, 0]
    target = destination[0]
    owner = target // TOK
    one_hot = (owner[:, None] == jnp.arange(DEV, dtype=jnp.int32)[None, :]).astype(jnp.int32)
    rank = jnp.sum(jnp.cumsum(one_hot, axis=0) * one_hot, axis=1) - 1
    slot = owner * CAP + rank
    table = jnp.stack([positions(seg, prefix), seg, slot, jnp.broadcast_to(prefix, seg.shape)])
    tables = jnp.stack([table, shift(table, "core", NC, 1)])
    pos, segs, slots, prefixes = (tables[:, k] for k in range(4))
    hit = slot[None, :] == jnp.arange(DEV * CAP, dtype=jnp.int32)[:, None]
    send_places = jnp.sum(jnp.where(hit, (target % TOK)[None, :], 0), axis=1)
    frequency = ROPE_BASE ** (
        -2.0 * jnp.arange(HEAD_DIM // 2, dtype=f32) / HEAD_DIM
    )
    angles = pos.astype(f32)[:, :, None] * frequency[None, None, :]
    cosine, sine = jnp.cos(angles), jnp.sin(angles)
    cosine = jnp.concatenate([cosine, cosine], axis=2)
    sine = jnp.concatenate([-sine, sine], axis=2)
    info = jnp.concatenate([core.reshape(1).astype(jnp.int32), prefixes[:, 0]])
    segc, segr, slots = segs[:, :, None], segs[:, None, :], slots[:, None, :]

    zi = lax.axis_index("dp").astype(jnp.int32)
    z_ab = (zi - jnp.array(OFFSETS_Z, jnp.int32)) % NZ
    lanes = (zi - jnp.array(OFFSETS_C, jnp.int32)) % NZ * (D // NZ)

    tie = lax.optimization_barrier
    c0 = lax.all_to_all(wc, chips, split_axis=0, concat_axis=0, tiled=True)
    c0 = c0.reshape(D // NZ, PART)
    up = shift(wab, "dp", NZ, 1)
    down = shift(wab, "dp", NZ, -1)
    far = shift(wab, "dp", NZ, 4)
    up2 = shift(jnp.stack([wab, up]), "dp", NZ, 2)
    down2 = shift(jnp.stack([wab, down]), "dp", NZ, -2)
    wz = assemble(z_ab, wab, up, down, far, up2, down2)
    wq = lax.all_gather(wz.reshape(NZ * 32, 2 * PART), chips, axis=0, tiled=True)

    c1 = [shift(c0, "dp", NZ, 1)]
    c1.append(shift(c0, "dp", NZ, -1))
    places = lax.all_to_all(
        send_places.reshape(DEV, CAP), plane, split_axis=0, concat_axis=0, tiled=True
    ).reshape(1, DEV * CAP)
    c2 = [shift(c1[0], "dp", NZ, 1)]
    c2.append(shift(c1[1], "dp", NZ, -1))
    c2, places = tie((c2, places))
    c3 = each(c2, "dp", NZ)
    c3, segc, segr, slots, info, cosine, sine = tie((c3, segc, segr, slots, info, cosine, sine))
    c4 = each([c3[0][:, :HALF], c3[1][:, HALF:]], "dp", NZ)
    cur = project_kv(lanes, own, other, c0, *c1, *c2, *c3, *c4, cosine, sine)
    onward = [(i, i + 1) for i in range(NCHIP - 1)]
    prev = []
    for h in range(2):
        prev.append(lax.ppermute(cur[h], chips, onward))
    wq = wq.reshape(NCHIP, NZ, 32, 2 * PART)

    whole = []
    for head in range(2):
        q = project_q(head, own, other, wq, cosine, sine)
        packed = attend(q, cur[head], prev[head], info, segc, segr, slots)
        got = lax.all_to_all(
            packed.reshape(DEV, NC * CAP, PART), plane, split_axis=0, concat_axis=0, tiled=True
        ).reshape(NCHIP, NC, NC * CAP, PART)
        whole = [place(places, got, head, whole)]
    return whole[0][None]


def solution(mesh):
    grid = Mesh(mesh.devices.reshape(NZ, NX, NY, NC), ("dp", "x", "y", "core"))
    seq = ("x", "y", "core")
    placed = (P("dp", seq, None), P(("dp", *seq), None), P("dp", seq), P("dp", seq), P("dp", seq))

    return jax.shard_map(
        on_device, mesh=grid, in_specs=placed, out_specs=P("dp", seq, None), check_vma=False
    )
```

```python
import jax
import jax.numpy as jnp
from jax import lax
from jax.experimental import pallas as pl
from jax.experimental.pallas import tpu as pltpu
from jax.sharding import Mesh, PartitionSpec as P


HEADS = 16
KV_HEADS = 4
HEAD_DIM = 128
REACH = 2
ROPE_BASE = 500000.0
MASKED = -1e30
LOG2E = 1.4426950408889634

NZ, NX, NY, NC = 8, 4, 4, 2
NCHIP = NX * NY
TOK = 384
CAP = 24
D = 4096
DEV = NCHIP * NC
PART = 512


bf16 = jnp.bfloat16
f32 = jnp.float32


def shift(x, axis, n, d):
    return lax.ppermute(x, axis, [(i, (i + d) % n) for i in range(n)])


OFFSETS_Z = (0, 1, 7, 4, 2, 3, 6, 5)
OFFSETS_C = (0, 1, 7, 2, 6, 3, 5, 4)


def each(pair, axis, n):
    return [shift(pair[0], axis, n, 1), shift(pair[1], axis, n, -1)]


def positions(segment_ids, prefix_len):
    index_list = jnp.arange(segment_ids.shape[0], dtype=jnp.int32)
    fresh_doc = jnp.concatenate([jnp.ones((1,), jnp.bool_), segment_ids[1:] != segment_ids[:-1]])
    first_row = lax.cummax(jnp.where(fresh_doc, index_list, 0), axis=0)
    leading = segment_ids == segment_ids[0]
    return index_list - first_row + jnp.where(leading, prefix_len, 0)


def split_kernel(core_ref, w_ref, mine_ref, theirs_ref):
    qw, kw = HEADS * HEAD_DIM // NC, KV_HEADS * HEAD_DIM // NC
    for ref, c in ((mine_ref, core_ref[0]), (theirs_ref, 1 - core_ref[0])):
        for h in range(2):
            for v in range(2):
                first = NC * qw + h * HEAD_DIM + v * NC * kw
                at = (2 * h + v) * HEAD_DIM
                ref[:, at : at + HEAD_DIM] = w_ref[
                    :, pl.ds(pl.multiple_of(first + c * kw, HEAD_DIM), HEAD_DIM)
                ]
        ref[:, PART:] = w_ref[:, pl.ds(pl.multiple_of(c * qw, HEAD_DIM), qw)]


def merge_kernel(core_ref, mine_ref, theirs_ref, c_ref, ab_ref):
    rows = mine_ref.shape[0]
    for ref, c in ((mine_ref, core_ref[0]), (theirs_ref, 1 - core_ref[0])):
        at = pl.ds(pl.multiple_of(c * rows, rows), rows)
        for p in range(NCHIP):
            c_ref[p, at, :] = ref[:, :PART]
        ab_ref[at, :] = ref[:, PART:]


def small_call(kernel, shapes, scalars, *arrays):
    vm = pl.BlockSpec(memory_space=pltpu.VMEM)
    return pl.pallas_call(
        kernel,
        out_shape=[jax.ShapeDtypeStruct(x, bf16) for x in shapes],
        in_specs=[pl.BlockSpec(memory_space=pltpu.SMEM)] + [vm] * len(arrays),
        out_specs=[vm] * len(shapes),
        cost_estimate=SMALL,
    )(scalars, *arrays)


def split(core_id, w):
    return small_call(split_kernel, [(16, 3 * PART)] * 2, core_id, w)


def merge(core_id, mine, theirs):
    return small_call(merge_kernel, [(NCHIP, 32, PART), (32, 2 * PART)], core_id, mine, theirs)


def assemble_kernel(zs_ref, one_ref, up_ref, down_ref, far_ref, up2_ref, down2_ref, out_ref):
    pieces = [one_ref[...], up_ref[...], down_ref[...], far_ref[...]]
    pieces += [r[k] for r in (up2_ref, down2_ref) for k in range(2)]
    for k, x in enumerate(pieces):
        out_ref[zs_ref[k]] = x


def assemble(zs, *pieces):
    vm = pl.BlockSpec(memory_space=pltpu.VMEM)
    return pl.pallas_call(
        assemble_kernel,
        out_shape=jax.ShapeDtypeStruct((NZ, 32, 2 * PART), bf16),
        in_specs=[pl.BlockSpec(memory_space=pltpu.SMEM)] + [vm] * len(pieces),
        out_specs=vm,
        cost_estimate=SMALL,
        name="assemble",
    )(zs, *pieces)


SMALL = pl.CostEstimate(flops=1 << 20, bytes_accessed=1 << 20, transcendentals=0)
HALF = PART // 2


def finish(acc, rotary, cos_ref, sin_ref, out_ref, b):
    for h in range(HALF // HEAD_DIM):
        x = acc[:, h * HEAD_DIM : (h + 1) * HEAD_DIM]
        if h < rotary:
            x = x * cos_ref[b] + pltpu.roll(x, HEAD_DIM // 2, 1) * sin_ref[b]
        out_ref[b, :, h * HEAD_DIM : (h + 1) * HEAD_DIM] = x.astype(bf16)


def project_kv_kernel(lane_ref, own_ref, other_ref, *refs):
    *w_refs, cos_ref, sin_ref, first_ref, second_ref = refs
    depth = D // NZ
    for n in range(2):
        cols = slice(n * HALF, (n + 1) * HALF)
        acc = None
        for k in range(NZ):
            w = w_refs[k][:, cols] if k < NZ - 1 else w_refs[NZ - 1 + n][...]
            at = pl.ds(pl.multiple_of(lane_ref[k], depth), depth)
            tok = jnp.concatenate([own_ref[:, at], other_ref[:, at]])
            term = jnp.dot(tok, w, preferred_element_type=f32)
            acc = term if acc is None else acc + term
        for b in range(2):
            rows = acc[b * TOK : (b + 1) * TOK]
            finish(rows, 1, cos_ref, sin_ref, (first_ref, second_ref)[n], b)


def project_kv(lanes, *arrays):
    vm = pl.BlockSpec(memory_space=pltpu.VMEM)
    return pl.pallas_call(
        project_kv_kernel,
        out_shape=[jax.ShapeDtypeStruct((2, TOK, HALF), bf16)] * 2,
        in_specs=[pl.BlockSpec(memory_space=pltpu.SMEM)] + [vm] * len(arrays),
        out_specs=[vm, vm],
        cost_estimate=SMALL,
        name="project_kv",
    )(lanes, *arrays)


def project_q_kernel(own_ref, other_ref, w_ref, cos_ref, sin_ref, out_ref):
    depth = D // NZ
    acc = None
    for z in range(NZ):
        w = w_ref[:, z].reshape(depth, HALF)
        at = slice(z * depth, (z + 1) * depth)
        tok = jnp.concatenate([own_ref[:, at], other_ref[:, at]])
        term = jnp.dot(tok, w, preferred_element_type=f32)
        acc = term if acc is None else acc + term
    for b in range(2):
        finish(acc[b * TOK : (b + 1) * TOK], 2, cos_ref, sin_ref, out_ref, b)


def project_q(head, own, other, w, cosine, sine):
    tok = pl.BlockSpec((TOK, D), lambda n: (0, 0))
    ang = pl.BlockSpec((2, TOK, HEAD_DIM), lambda n: (0, 0, 0))
    return pl.pallas_call(
        project_q_kernel,
        out_shape=jax.ShapeDtypeStruct((2, TOK, PART), bf16),
        grid=(2,),
        in_specs=[
            tok, tok, pl.BlockSpec((NCHIP, NZ, 32, HALF), lambda n: (0, 0, 0, 2 * head + n)), ang, ang
        ],
        out_specs=pl.BlockSpec((2, TOK, HALF), lambda n: (0, 0, n)),
        cost_estimate=SMALL,
        name="project_q",
    )(own, other, w, cosine, sine)


GROUP = HEADS // KV_HEADS
TILE = 128


def attend_kernel(
    info_ref, q_ref, cur_ref, prev_ref, segr_ref, slot_ref, out_ref, kv_ref, bias_ref, rows_ref
):
    b = pl.program_id(0)
    core = info_ref[0]
    i = jnp.bitwise_xor(core, b)
    span = REACH * TOK

    @pl.when(b == 0)
    def _():
        for n in range(2):
            k = jnp.bitwise_xor(core, n)
            for m, ref in ((n, prev_ref), (2 + n, cur_ref)):
                kv_ref[m, :, : 2 * HEAD_DIM] = ref[k]
                kv_ref[m, :, 2 * HEAD_DIM :] = jnp.ones((TOK, HEAD_DIM), bf16)

    prefix = info_ref[1 + i]
    segr = segr_ref[i]
    segc = jnp.broadcast_to(segr.astype(f32), (128, TOK)).T[:, :1].astype(jnp.int32)
    leading = segc == segr[:, :1]
    row = lax.broadcasted_iota(jnp.int32, (TOK, TOK), 0)
    col = lax.broadcasted_iota(jnp.int32, (TOK, TOK), 1)
    bias_ref[:, span:] = jnp.where((col <= row) & (segc == segr), 0.0, MASKED)
    rcol = lax.broadcasted_iota(jnp.int32, (TOK, span), 1) - span
    bias_ref[:, :span] = jnp.where((rcol >= -prefix) & leading, 0.0, MASKED)

    keys = kv_ref[pl.ds(b, 3), :, :HEAD_DIM].reshape(3 * TOK, HEAD_DIM)
    vals = kv_ref[pl.ds(b, 3), :, HEAD_DIM:].reshape(3 * TOK, 2 * HEAD_DIM)
    for r in range(TOK // TILE):
        rows = slice(r * TILE, (r + 1) * TILE)
        n = span + (r + 1) * TILE
        for g in range(GROUP):
            cols = slice(g * HEAD_DIM, (g + 1) * HEAD_DIM)
            s = lax.dot_general(
                q_ref[i, rows, cols], keys[:n], (((1,), (1,)), ((), ())), preferred_element_type=f32
            )
            s = s * (HEAD_DIM**-0.5 * LOG2E) + bias_ref[rows, :n]
            e = jnp.exp2(s - jnp.max(s, axis=1, keepdims=True)).astype(bf16)
            o = jnp.dot(e, vals[:n], preferred_element_type=f32)
            rows_ref[rows, cols] = (o[:, :HEAD_DIM] / o[:, HEAD_DIM:]).astype(bf16)

    slots = lax.broadcasted_iota(jnp.int32, (DEV * CAP, TOK), 0)
    pick = jnp.where(slots == slot_ref[i], 1.0, 0.0).astype(bf16)
    packed = jnp.dot(pick, rows_ref[...], preferred_element_type=f32)
    out_ref[:, 0] = packed.reshape(DEV, CAP, GROUP * HEAD_DIM).astype(bf16)


def attend(q, cur, prev, info, segr, slot):
    width = GROUP * HEAD_DIM

    def whole(x):
        return pl.BlockSpec(x.shape, lambda b, info: (0,) * x.ndim)

    return pl.pallas_call(
        attend_kernel,
        out_shape=jax.ShapeDtypeStruct((DEV, 2, CAP, width), bf16),
        grid_spec=pltpu.PrefetchScalarGridSpec(
            num_scalar_prefetch=1,
            grid=(2,),
            in_specs=[
                whole(q), whole(cur), whole(prev), whole(segr), whole(slot),
            ],
            out_specs=pl.BlockSpec((DEV, 1, CAP, width), lambda b, info: (0, b, 0, 0)),
            scratch_shapes=[
                pltpu.VMEM((4, TOK, 3 * HEAD_DIM), bf16),
                pltpu.VMEM((TOK, 3 * TOK), f32),
                pltpu.VMEM((TOK, width), bf16),
            ],
        ),
        cost_estimate=SMALL,
        name="attend",
    )(info, q, cur, prev, segr, slot)


def place_kernel(places_ref, got_ref, *refs):
    out_ref, pick_ref = refs[-2:]

    @pl.when(pl.program_id(0) == 0)
    def _():
        rows = lax.broadcasted_iota(jnp.int32, (TOK, DEV * CAP), 0)
        pick_ref[...] = jnp.where(rows == places_ref[...], 1.0, 0.0).astype(bf16)

    out_ref[...] = jnp.dot(
        pick_ref[...], got_ref[...].reshape(DEV * CAP, PART), preferred_element_type=f32
    ).astype(bf16)


def place(places, got, head, whole):
    return pl.pallas_call(
        place_kernel,
        out_shape=jax.ShapeDtypeStruct((TOK, HEADS * HEAD_DIM), bf16),
        grid=(NC,),
        in_specs=[
            pl.BlockSpec((1, DEV * CAP), lambda c: (0, 0)),
            pl.BlockSpec((NCHIP, 1, NC * CAP, PART), lambda c: (0, c, 0, 0)),
        ]
        + [pl.BlockSpec(memory_space=pl.ANY)] * len(whole),
        out_specs=pl.BlockSpec((TOK, PART), lambda c: (0, 2 * c + head)),
        scratch_shapes=[pltpu.VMEM((TOK, DEV * CAP), bf16)],
        input_output_aliases={2: 0} if whole else {},
        cost_estimate=SMALL,
        name="place",
    )(places, got, *whole)


def on_device(tokens, qkv_weight, segments, destination, doc_prefix):
    own = tokens[0]
    core = lax.axis_index("core")
    plane = ("x", "y", "core")
    chips = ("x", "y")

    core_id = core.reshape(1).astype(jnp.int32)
    mine, theirs = split(core_id, qkv_weight)
    wc, wab = merge(core_id, mine, shift(theirs, "core", NC, 1))
    other = shift(own, "core", NC, 1)

    seg = segments[0]
    prefix = doc_prefix[0, 0]
    target = destination[0]
    owner = target // TOK
    one_hot = (owner[:, None] == jnp.arange(DEV, dtype=jnp.int32)[None, :]).astype(jnp.int32)
    rank = jnp.sum(jnp.cumsum(one_hot, axis=0) * one_hot, axis=1) - 1
    slot = owner * CAP + rank
    table = jnp.stack([positions(seg, prefix), seg, slot, jnp.broadcast_to(prefix, seg.shape)])
    tables = jnp.stack([table, shift(table, "core", NC, 1)])
    pos, segs, slots, prefixes = (tables[:, k] for k in range(4))
    hit = slot[None, :] == jnp.arange(DEV * CAP, dtype=jnp.int32)[:, None]
    send_places = jnp.sum(jnp.where(hit, (target % TOK)[None, :], 0), axis=1)
    frequency = ROPE_BASE ** (
        -2.0 * jnp.arange(HEAD_DIM // 2, dtype=f32) / HEAD_DIM
    )
    angles = pos.astype(f32)[:, :, None] * frequency[None, None, :]
    cosine, sine = jnp.cos(angles), jnp.sin(angles)
    cosine = jnp.concatenate([cosine, cosine], axis=2)
    sine = jnp.concatenate([-sine, sine], axis=2)
    info = jnp.concatenate([core.reshape(1).astype(jnp.int32), prefixes[:, 0]])
    segr, slots = segs[:, None, :], slots[:, None, :]

    zi = lax.axis_index("dp").astype(jnp.int32)
    z_ab = (zi - jnp.array(OFFSETS_Z, jnp.int32)) % NZ
    lanes = (zi - jnp.array(OFFSETS_C, jnp.int32)) % NZ * (D // NZ)

    tie = lax.optimization_barrier
    c0 = lax.all_to_all(wc, chips, split_axis=0, concat_axis=0, tiled=True)
    c0 = c0.reshape(D // NZ, PART)
    up = shift(wab, "dp", NZ, 1)
    down = shift(wab, "dp", NZ, -1)
    far = shift(wab, "dp", NZ, 4)
    up2 = shift(jnp.stack([wab, up]), "dp", NZ, 2)
    down2 = shift(jnp.stack([wab, down]), "dp", NZ, -2)
    wz = assemble(z_ab, wab, up, down, far, up2, down2)
    wq = lax.all_gather(wz.reshape(NZ * 32, 2 * PART), chips, axis=0, tiled=True)

    c1 = [shift(c0, "dp", NZ, 1)]
    c1.append(shift(c0, "dp", NZ, -1))
    places = lax.all_to_all(
        send_places.reshape(DEV, CAP), plane, split_axis=0, concat_axis=0, tiled=True
    ).reshape(1, DEV * CAP)
    c2 = [shift(c1[0], "dp", NZ, 1)]
    c2.append(shift(c1[1], "dp", NZ, -1))
    c2, places = tie((c2, places))
    c3 = each(c2, "dp", NZ)
    c3, segr, slots, info, cosine, sine = tie((c3, segr, slots, info, cosine, sine))
    c4 = each([c3[0][:, :HALF], c3[1][:, HALF:]], "dp", NZ)
    cur = project_kv(lanes, own, other, c0, *c1, *c2, *c3, *c4, cosine, sine)
    onward = [(i, i + 1) for i in range(NCHIP - 1)]
    prev = []
    for h in range(2):
        prev.append(lax.ppermute(cur[h], chips, onward))
    wq = wq.reshape(NCHIP, NZ, 32, 2 * PART)

    whole = []
    for head in range(2):
        q = project_q(head, own, other, wq, cosine, sine)
        packed = attend(q, cur[head], prev[head], info, segr, slots)
        got = lax.all_to_all(
            packed.reshape(DEV, NC * CAP, PART), plane, split_axis=0, concat_axis=0, tiled=True
        ).reshape(NCHIP, NC, NC * CAP, PART)
        whole = [place(places, got, head, whole)]
    return whole[0][None]


def solution(mesh):
    grid = Mesh(mesh.devices.reshape(NZ, NX, NY, NC), ("dp", "x", "y", "core"))
    seq = ("x", "y", "core")
    placed = (P("dp", seq, None), P(("dp", *seq), None), P("dp", seq), P("dp", seq), P("dp", seq))

    return jax.shard_map(
        on_device, mesh=grid, in_specs=placed, out_specs=P("dp", seq, None), check_vma=False
    )
```
